32 devices in a mesh: groups: 2 (over x), seq: 16 (over z, y, core).
Axes of the slice: x: 2, y: 2, z: 4, core: 2. Of those that a mesh axis runs over, the one named last changes fastest.
Arguments:
- queries: bfloat16 [16384, 2048], P(('groups', 'seq')), parts along dimension 0, may hold values from -10 to 10
- keys: bfloat16 [16384, 2048], P(('groups', 'seq')), parts along dimension 0, may hold values from -10 to 10
- values: bfloat16 [16384, 2048], P(('groups', 'seq')), parts along dimension 0, may hold values from -6 to 6
- ssd_input: bfloat16 [16384, 2048], P(('groups', 'seq')), parts along dimension 0, may hold values from -6 to 6
- bmat: bfloat16 [16384, 128], P(('groups', 'seq')), parts along dimension 0, may hold values from -0.5 to 0.5
- cmat: bfloat16 [16384, 128], P(('groups', 'seq')), parts along dimension 0, may hold values from -6 to 6
- expo: int32 [16384, 32], P(('groups', 'seq')), parts along dimension 0, may hold values from 1 to 16384
- rate: float32 [32], replicated, may hold values from 1.2207031e-05 to 0.06
- skip: float32 [32], replicated, may hold values from 0.5 to 1.5
Outputs:
- attn_out: bfloat16 [16384, 2048], P(('groups', 'seq')), parts along dimension 0
- normed_recurrence_output: bfloat16 [16384, 2048], P(('groups', 'seq')), parts along dimension 0
The draws below stay inside these ranges and needn't reach their ends.
There are 2 independent parts, one for each index of `groups`. The reference program is written for one: setup_inputs(seed, part) draws one part's arguments, and reference() takes and returns one part's arrays. A program takes and returns all parts, laid end to end along the dimension named above; an argument that names none is the same for every part. Nothing has to cross between parts.
All inputs are finite; a program needn't handle non-finite values.
Results may differ from the reference program's by a relative error of at most 0.0049.
Values may be sent and summed in bfloat16 or wider, within the bound.
A program may use at most 192 MiB of HBM per device.

```python
import math
import jax
import jax.numpy as jnp
from jax import lax

HA = 16
E = 128
W = 2048
HS = 32
P_SIZE = 64
N = 128
Q = 256
DOCUMENT_LENGTH = 8192


def draw_queries(key, part):
    drawn = jnp.clip(1.6 * jax.random.normal(jax.random.fold_in(key, 1), (DOCUMENT_LENGTH, HA * E), jnp.float32), -10.0, 10.0)
    return drawn.astype(jnp.bfloat16)


def draw_keys(key, part):
    drawn = jnp.clip(1.6 * jax.random.normal(jax.random.fold_in(key, 2), (DOCUMENT_LENGTH, HA * E), jnp.float32), -10.0, 10.0)
    return drawn.astype(jnp.bfloat16)


def draw_expo(key, part):
    random_base_key, spike_random_key = jax.random.split(jax.random.fold_in(key, 11))
    base_values_list = jax.random.randint(random_base_key, (DOCUMENT_LENGTH, HS), 1, 4)
    spike_positions = jax.random.randint(spike_random_key, (4,), 0, DOCUMENT_LENGTH)
    spike_row_list = jnp.any(jnp.arange(DOCUMENT_LENGTH)[:, None] == spike_positions[None, :], axis=1)
    return jnp.where(spike_row_list[:, None], 2 * DOCUMENT_LENGTH, base_values_list).astype(jnp.int32)


def draw_rate(key, part):
    slow_key, fast_key, pick_key = jax.random.split(jax.random.fold_in(key, 13), 3)
    slow_rate = jnp.exp(jax.random.uniform(slow_key, (HS,), jnp.float32, math.log(0.1), math.log(0.22))) / DOCUMENT_LENGTH
    fast_rate = jnp.exp(jax.random.uniform(fast_key, (HS,), jnp.float32, math.log(0.02), math.log(0.06)))
    fast_heads = jax.random.uniform(pick_key, (HS,)) < 0.5
    return jnp.where(fast_heads, fast_rate, slow_rate).astype(jnp.float32)


def block_levels(own_key, dims, pieces, low, top_value):
    factor_of = 1.0
    for position, blocks in pieces:
        steps = jax.random.uniform(jax.random.fold_in(jax.random.fold_in(own_key, 6), position), (blocks,), jnp.float32, low / len(pieces), top_value / len(pieces))
        factor_of = factor_of * jnp.repeat(jnp.exp(steps), dims[position] // blocks).reshape((-1,) + (1,) * (len(dims) - 1 - position))
    return factor_of


def centred(stream_key, shape, scale, limit, cuts=(), kind=jnp.bfloat16):
    entries = scale * jax.random.normal(stream_key, shape, jnp.float32)
    if cuts:
        entries = entries * block_levels(stream_key, shape, cuts, -0.22, 0.18)
    return jnp.clip(entries, -limit, limit).astype(kind)


def setup_inputs(seed: int = 0, part: int = 0) -> dict:
    arg_keys = jax.random.split(jax.random.key(seed), 10)
    part_keys = jax.random.split(jax.random.fold_in(arg_keys[9], part), 10)
    queries = draw_queries(jax.random.fold_in(jax.random.fold_in(arg_keys[9], part), 71), part)
    keys = draw_keys(jax.random.fold_in(jax.random.fold_in(arg_keys[9], part), 71), part)
    values = centred(part_keys[2], (DOCUMENT_LENGTH, HA * E), 1.0, 6.0, ((0, 16),))
    ssd_input = centred(part_keys[3], (DOCUMENT_LENGTH, HS * P_SIZE), 1.0, 6.0, ((0, 16),))
    bmat = centred(part_keys[4], (DOCUMENT_LENGTH, N), N ** -0.5, 0.5, ((0, 16),))
    cmat = centred(part_keys[5], (DOCUMENT_LENGTH, N), 1.0, 6.0, ((0, 16),))
    expo = draw_expo(jax.random.fold_in(jax.random.fold_in(arg_keys[9], part), 71), part)
    rate = draw_rate(jax.random.fold_in(arg_keys[9], 71), part)
    skip = jnp.clip(jax.random.uniform(arg_keys[8], (HS,), jnp.float32, 0.5, 1.5), 0.5, 1.5)
    return {"queries": queries, "keys": keys, "values": values, "ssd_input": ssd_input, "bmat": bmat, "cmat": cmat, "expo": expo, "rate": rate, "skip": skip}


def block_local(piece_x, piece_b, piece_c, piece_loga):
    cumulative = jnp.cumsum(piece_loga, axis=0).T
    block_len = cumulative.shape[1]
    lower_mask = jnp.arange(block_len)[:, None] >= jnp.arange(block_len)[None, :]
    log_gaps = cumulative[:, :, None] - cumulative[:, None, :]
    decay_grid = jnp.where(lower_mask[None], jnp.exp(jnp.where(lower_mask[None], log_gaps, 0.0)), 0.0)
    cross_term = jnp.dot(piece_c, piece_b.T, preferred_element_type=jnp.float32)
    inner_term = (cross_term[None] * decay_grid).astype(jnp.bfloat16)
    intra_term = jnp.einsum('hts,shp->thp', inner_term.astype(jnp.float32), piece_x.astype(jnp.float32))
    end_weights = jnp.exp(cumulative[:, -1:] - cumulative)
    weighted = (end_weights.T[:, :, None] * piece_b.astype(jnp.float32)[:, None, :]).astype(jnp.bfloat16)
    local_state = jnp.einsum('shp,shn->hpn', piece_x.astype(jnp.float32), weighted.astype(jnp.float32))
    end_decay = jnp.exp(cumulative[:, -1])
    return (intra_term, cumulative, end_decay, local_state)

def block_output(intra_term, cumulative, piece_x, piece_c, skip, carried):
    inter_term = jnp.einsum('tn,hpn->thp', piece_c.astype(jnp.float32), carried, precision=lax.Precision.HIGHEST)
    mixed = intra_term + inter_term * jnp.exp(cumulative.T)[:, :, None] + skip[None, :, None] * piece_x.astype(jnp.float32)
    inv_rms = lax.rsqrt(lax.optimization_barrier(jnp.mean(mixed * mixed, axis=2, keepdims=True)) + 1e-05)
    return (mixed * inv_rms).astype(jnp.bfloat16).reshape(mixed.shape[0], mixed.shape[1] * mixed.shape[2])

def recurrence_ref(ssd_input, bmat, cmat, expo, rate, skip):
    block_count = DOCUMENT_LENGTH // Q
    all_x = ssd_input.reshape(block_count, Q, HS, P_SIZE)
    all_loga = (-rate[None, :] * expo.astype(jnp.float32)).reshape(block_count, Q, HS)
    all_b = bmat.reshape(block_count, Q, N)
    all_c = cmat.reshape(block_count, Q, N)

    def advance(carried, slices):
        piece_x, piece_b, piece_c, piece_loga = slices
        intra_term, cumulative, end_decay, local_state = block_local(piece_x, piece_b, piece_c, piece_loga)
        result = block_output(intra_term, cumulative, piece_x, piece_c, skip, carried)
        return (end_decay[:, None, None] * carried + local_state, result)
    start_state = jnp.zeros((HS, P_SIZE, N), jnp.float32)
    closing_state, outputs = lax.scan(advance, start_state, (all_x, all_b, all_c, all_loga))
    return outputs.reshape(DOCUMENT_LENGTH, HS * P_SIZE)

def attention_ref(queries, keys, values):
    block_rows = math.gcd(DOCUMENT_LENGTH, 512)
    zero_rows = jnp.zeros((W, HA * E), keys.dtype)
    keys_pad = jnp.concatenate([zero_rows, keys], axis=0)
    values_pad = jnp.concatenate([zero_rows, values], axis=0)

    def one_block(block_index):
        block_start = (block_index * block_rows).astype(jnp.int32)
        query_blk = lax.dynamic_slice_in_dim(queries, block_start, block_rows, 0).reshape(block_rows, HA, E).astype(jnp.float32)
        key_blk = lax.dynamic_slice_in_dim(keys_pad, block_start, block_rows + W, 0).reshape(block_rows + W, HA, E).astype(jnp.float32)
        value_blk = lax.dynamic_slice_in_dim(values_pad, block_start, block_rows + W, 0).reshape(block_rows + W, HA, E).astype(jnp.float32)
        query_pos = block_start + jnp.arange(block_rows, dtype=jnp.int32)
        key_pos = block_start - W + jnp.arange(block_rows + W, dtype=jnp.int32)
        visible = (key_pos[None, :] <= query_pos[:, None]) & (key_pos[None, :] > query_pos[:, None] - W) & (key_pos[None, :] >= 0)
        scores = jnp.einsum('rhe,khe->hrk', query_blk, key_blk) / math.sqrt(E)
        scores = jnp.where(visible[None], scores, -1e+30)
        row_max = lax.optimization_barrier(jnp.max(scores, axis=2, keepdims=True))
        exp_scores = jnp.exp(scores - row_max)
        attn_probs = (exp_scores / lax.optimization_barrier(jnp.sum(exp_scores, axis=2, keepdims=True))).astype(jnp.bfloat16)
        block_out = jnp.einsum('hrk,khe->rhe', attn_probs.astype(jnp.float32), value_blk)
        return block_out.reshape(block_rows, HA * E).astype(jnp.bfloat16)
    outputs = lax.map(one_block, jnp.arange(DOCUMENT_LENGTH // block_rows, dtype=jnp.int32))
    return outputs.reshape(DOCUMENT_LENGTH, HA * E)

def reference(queries, keys, values, ssd_input, bmat, cmat, expo, rate, skip):
    attn_out = attention_ref(queries, keys, values)
    normed_recurrence_output = recurrence_ref(ssd_input, bmat, cmat, expo, rate, skip)
    return (attn_out, normed_recurrence_output)
```

```python
import functools
import math

import jax
import jax.numpy as jnp
from jax import lax
from jax.experimental import pallas as pl
from jax.experimental.pallas import tpu as pltpu
from jax.sharding import PartitionSpec as P

E = 128
W = 2048
Q = 256
CHUNKS = 4
NEG = -1e30
LOG2E = math.log2(math.e)


def dot(a, b):
    return jnp.dot(a, b, preferred_element_type=jnp.float32)


def dot_t(a, b):
    return lax.dot_general(a, b, (((1,), (1,)), ((), ())), preferred_element_type=jnp.float32)


def attention_kernel(bias_ref, q_ref, ko_ref, vo_ref, *refs):
    pairs = [(refs[2 * i], refs[2 * i + 1]) for i in range(4)]
    out_ref = refs[8]
    length = q_ref.shape[0]
    tq = min(256, length)
    scale = LOG2E / math.sqrt(E)
    row = lax.broadcasted_iota(jnp.int32, (tq, tq), 0)
    col = lax.broadcasted_iota(jnp.int32, (tq, tq), 1)
    for r in range(0, length, tq):
        q = q_ref[r : r + tq, :]
        tiles = []
        tiles.append((ko_ref, vo_ref, r, tq, "low", None))
        if r > 0:
            tiles.append((ko_ref, vo_ref, 0, r, None, None))
        kz, vz = pairs[0]
        tiles.append((kz, vz, r, tq, "up", 0))
        if r + tq < length:
            tiles.append((kz, vz, r + tq, length - r - tq, None, 0))
        for n in range(1, 4):
            tiles.append((pairs[n][0], pairs[n][1], 0, length, None, n))
        m = l = acc = None
        for k_ref, v_ref, start, size, mask, slot in tiles:
            s = dot_t(q, k_ref[start : start + size, :]) * scale
            if mask == "low":
                s = jnp.where(col <= row, s, NEG)
            elif mask == "up":
                s = jnp.where(col > row, s, NEG)
            peak = jnp.max(s, axis=1, keepdims=True)
            if slot is not None:
                bias = bias_ref[slot]
                peak = peak + bias
            m_new = peak if m is None else jnp.maximum(m, peak)
            shift = m_new if slot is None else m_new - bias
            p = jnp.exp2(s - shift)
            total = jnp.sum(p, axis=1, keepdims=True)
            part = dot(p.astype(jnp.bfloat16), v_ref[start : start + size, :])
            if m is None:
                l, acc = total, part
            else:
                alpha = jnp.exp2(m - m_new)
                l = l * alpha + total
                acc = acc * alpha + part
            m = m_new
        out_ref[r : r + tq, :] = (acc / l).astype(out_ref.dtype)


def attention_chunk(bias, queries, keys, values, shards, chunk, heads):
    length = queries.shape[0]
    first = chunk * heads

    def cols(offset):
        return pl.BlockSpec((length, E), lambda h: (0, h + offset))

    specs = [pl.BlockSpec(memory_space=pltpu.SMEM), cols(first), cols(first), cols(first)]
    args = [bias, queries, keys, values]
    for shard in shards:
        specs += [cols(0), cols(heads)]
        args += [shard, shard]
    work = heads * length * (length + W)
    return pl.pallas_call(
        attention_kernel,
        grid=(heads,),
        in_specs=specs,
        out_specs=cols(0),
        out_shape=jax.ShapeDtypeStruct((length, heads * E), jnp.bfloat16),
        compiler_params=pltpu.CompilerParams(vmem_limit_bytes=48 << 20),
        cost_estimate=pl.CostEstimate(
            flops=4 * work * E, transcendentals=work, bytes_accessed=12 * length * heads * E * 2
        ),
        name="window_attention",
    )(*args)


def pair_columns(lane, table, j, width):
    return jnp.where(lane < width, table[:, 2 * j : 2 * j + 1], table[:, 2 * j + 1 : 2 * j + 2])


def state_kernel(x_ref, bt_ref, end_ref, local_ref):
    rows, total_cols = x_ref.shape
    head_count = end_ref.shape[1]
    width = total_cols // head_count
    lane = lax.broadcasted_iota(jnp.int32, (1, 2 * width), 1)
    for block in range(rows // Q):
        r = block * Q
        weights = jnp.exp(end_ref[r : r + Q, :])
        bt = bt_ref[:, r : r + Q]
        for j in range(head_count // 2):
            cs = slice(2 * width * j, 2 * width * (j + 1))
            xs = x_ref[r : r + Q, cs].astype(jnp.float32) * pair_columns(lane, weights, j, width)
            local_ref[block, :, cs] = dot(bt, xs.astype(jnp.bfloat16))


def output_kernel(x_ref, b_ref, c_ref, cum_ref, cumt_ref, skip_ref, carried_ref, local_ref, decay_ref, out_ref):
    rows, total_cols = x_ref.shape
    head_count = cum_ref.shape[1]
    width = total_cols // head_count
    pair = 2 * width
    lane = lax.broadcasted_iota(jnp.int32, (1, pair), 1)
    low = lax.broadcasted_iota(jnp.int32, (Q, Q), 1) <= lax.broadcasted_iota(jnp.int32, (Q, Q), 0)
    same = (lax.broadcasted_iota(jnp.int32, (pair, pair), 0) < width) == (
        lax.broadcasted_iota(jnp.int32, (pair, pair), 1) < width
    )
    ones = jnp.where(same, 1.0, 0.0).astype(jnp.bfloat16)
    for block in range(rows // Q):
        r = block * Q
        c = c_ref[r : r + Q, :]
        cross = jnp.where(low, dot_t(c, b_ref[r : r + Q, :]), 0.0)
        cum = cum_ref[r : r + Q, :]
        grown = jnp.exp(cum)
        for j in range(head_count // 2):
            cs = slice(pair * j, pair * (j + 1))
            x = x_ref[r : r + Q, cs]
            intra = []
            for h in (2 * j, 2 * j + 1):
                gap = cum[:, h : h + 1] - cumt_ref[h : h + 1, r : r + Q]
                grid = jnp.exp(jnp.minimum(gap, 0.0))
                intra.append(dot((cross * grid).astype(jnp.bfloat16), x))
            carried = carried_ref[:, cs].astype(jnp.float32)
            for b in range(block):
                carried = carried * decay_ref[b : b + 1, cs] + local_ref[b, :, cs]
            high = carried.astype(jnp.bfloat16)
            rest = (carried - high.astype(jnp.float32)).astype(jnp.bfloat16)
            inter = dot(c, high) + dot(c, rest)
            mixed = (
                jnp.where(lane < width, intra[0], intra[1])
                + inter * pair_columns(lane, grown, j, width)
                + skip_ref[:, cs] * x.astype(jnp.float32)
            )
            square = mixed * mixed
            big = square.astype(jnp.bfloat16)
            small = (square - big.astype(jnp.float32)).astype(jnp.bfloat16)
            mean = (dot(big, ones) + dot(small, ones)) * (1.0 / width)
            out_ref[r : r + Q, cs] = (mixed * lax.rsqrt(mean + 1e-05)).astype(out_ref.dtype)


def whole_spec(array):
    return pl.BlockSpec(array.shape, lambda: (0,) * array.ndim)


def call_whole(kernel, args, out, name, flops):
    return pl.pallas_call(
        kernel,
        in_specs=[whole_spec(a) for a in args],
        out_specs=whole_spec(out),
        out_shape=out,
        compiler_params=pltpu.CompilerParams(vmem_limit_bytes=48 << 20),
        cost_estimate=pl.CostEstimate(flops=flops, transcendentals=0, bytes_accessed=6 << 20),
        name=name,
    )(*args)


def pick(options, index):
    result = options[0]
    for n in range(1, len(options)):
        result = jnp.where(index == n, options[n], result)
    return result


def swap(value, size, bit):
    return lax.ppermute(value, "seq", [(i, i ^ bit) for i in range(size)])


def entering_state(total, decay, size, here):
    member = here % 4
    quad = here // 4
    group = total.shape[1] // 4
    heads = decay.shape[0]
    width = total.shape[1] // heads

    def own_columns(which):
        return lax.dynamic_slice_in_dim(total, which * group, group, 1)

    states = [own_columns(member)]
    decays = [decay]
    for bit in (1, 2, 3):
        sent = own_columns(member ^ bit).astype(jnp.bfloat16)
        states.append(swap(sent, size, bit).astype(jnp.float32))
        decays.append(swap(decay, size, bit))
    state_of = [pick(states, j ^ member) for j in range(4)]
    decay_of = []
    for j in range(4):
        d = lax.dynamic_slice_in_dim(pick(decays, j ^ member), member * (heads // 4), heads // 4, 0)
        decay_of.append(jnp.repeat(d, width)[None, :])
    sum_q = state_of[0]
    decay_q = decay_of[0]
    for j in range(1, 4):
        sum_q = sum_q * decay_of[j] + state_of[j]
        decay_q = decay_q * decay_of[j]
    entry = jnp.zeros_like(sum_q)
    for step in range(1, size // 4):
        route = [(4 * (step - 1) + j, 4 * step + j) for j in range(4)]
        got = lax.ppermute(entry * decay_q + sum_q, "seq", route)
        entry = jnp.where(quad == step, got, entry)
    carried_of = [entry]
    for j in range(3):
        carried_of.append(carried_of[-1] * decay_of[j] + state_of[j])
    back = [pick(carried_of, member).astype(jnp.bfloat16)]
    for bit in (1, 2, 3):
        back.append(swap(pick(carried_of, member ^ bit).astype(jnp.bfloat16), size, bit))
    return jnp.concatenate([pick(back, g ^ member) for g in range(4)], axis=1)


def on_device(queries, keys, values, ssd_input, bmat, cmat, expo, rate, skip):
    length = queries.shape[0]
    size = lax.axis_size("seq")
    here = lax.axis_index("seq")
    quad = here // 4
    row = (here // 2) % 2
    core = here % 2
    head_total = queries.shape[1] // E
    heads = head_total // CHUNKS
    cw = heads * E

    own = []
    for n in range(CHUNKS):
        cs = slice(n * cw, (n + 1) * cw)
        own.append(jnp.concatenate([keys[:, cs], values[:, cs]], axis=1))
    route = [(i, i + 4) for i in range(size - 4)]
    from_z = [lax.ppermute(part, "seq", route) for part in own]

    head_count = rate.shape[0]
    width = ssd_input.shape[1] // head_count
    blocks = length // Q
    loga = -rate[None, :] * expo.astype(jnp.float32)
    cum3 = jnp.cumsum(loga.reshape(blocks, Q, head_count), axis=1)
    ends = cum3[:, -1, :]
    cum = cum3.reshape(length, head_count)
    end_gap = (ends[:, None, :] - cum3).reshape(length, head_count)
    end_decay = jnp.exp(ends)
    decay_cols = jnp.repeat(end_decay, width, axis=1)
    local = call_whole(
        state_kernel,
        (ssd_input, bmat.T, end_gap),
        jax.ShapeDtypeStruct((blocks, cmat.shape[1], ssd_input.shape[1]), jnp.float32),
        "local_states",
        2 * length * cmat.shape[1] * ssd_input.shape[1],
    )
    dev_state = local[0]
    dev_decay = end_decay[0]
    for b in range(1, blocks):
        dev_state = dev_state * decay_cols[b : b + 1] + local[b]
        dev_decay = dev_decay * end_decay[b]
    carried = entering_state(dev_state, dev_decay, size, here)
    recurrence = call_whole(
        output_kernel,
        (
            ssd_input,
            bmat,
            cmat,
            cum,
            cum.T,
            jnp.repeat(skip, width)[None, :],
            carried,
            local,
            decay_cols,
        ),
        jax.ShapeDtypeStruct(ssd_input.shape, jnp.bfloat16),
        "recurrence_output",
        8 * length * Q * ssd_input.shape[1],
    )

    inside = quad > 0
    valid = [inside, inside | (row == 1), inside | (row == 1), inside | (core == 1)]
    bias = jnp.stack([jnp.where(v, 0.0, NEG) for v in valid]).astype(jnp.float32)
    results = []
    for n in range(CHUNKS):
        by_row = swap(jnp.where(row == 0, own[n], from_z[n]), size, 2)
        by_core = swap(by_row, size, 1)
        near = swap(jnp.where(core == 0, own[n], from_z[n]), size, 1)
        results.append(
            attention_chunk(
                bias, queries, keys, values, (from_z[n], by_row, by_core, near), n, heads
            )
        )
    return (jnp.concatenate(results, axis=1), recurrence)


def solution(mesh):
    split = P(("groups", "seq"), None)
    return jax.shard_map(
        on_device,
        mesh=mesh,
        in_specs=(split,) * 7 + (P(), P()),
        out_specs=(split, split),
        check_vma=False,
    )
```

```python
import functools
import math

import jax
import jax.numpy as jnp
from jax import lax
from jax.experimental import pallas as pl
from jax.experimental.pallas import tpu as pltpu
from jax.sharding import PartitionSpec as P

E = 128
W = 2048
Q = 256
CHUNK = 256
AHEAD = 3
NEG = -1e30
LOG2E = math.log2(math.e)
MESH = pl.DeviceIdType.MESH
Z, Y, A, B = range(4)


def dot(a, b):
    return jnp.dot(a, b, preferred_element_type=jnp.float32)


def dot_t(a, b):
    return lax.dot_general(a, b, (((1,), (1,)), ((), ())), preferred_element_type=jnp.float32)


def attend(bias, q_ref, ko_ref, vo_ref, held, out_ref, chunk):
    length = q_ref.shape[0]
    tq = min(256, length)
    scale = LOG2E / math.sqrt(E)
    row = lax.broadcasted_iota(jnp.int32, (tq, tq), 0)
    col = lax.broadcasted_iota(jnp.int32, (tq, tq), 1)
    for head in range(CHUNK // E):
        wide = pl.ds(pl.multiple_of(chunk * CHUNK + head * E, E), E)
        near = slice(head * E, (head + 1) * E)
        for r in range(0, length, tq):
            q = q_ref[r : r + tq, wide]
            tiles = [(None, r, tq, "low")]
            if r > 0:
                tiles.append((None, 0, r, None))
            tiles.append((Z, r, tq, "up"))
            if r + tq < length:
                tiles.append((Z, r + tq, length - r - tq, None))
            tiles += [(n, 0, length, None) for n in (Y, A, B)]
            m = l = acc = None
            for kind, start, size, mask in tiles:
                rows = slice(start, start + size)
                if kind is None:
                    k, v = ko_ref[rows, wide], vo_ref[rows, wide]
                else:
                    k, v = held[kind, chunk, 0, rows, near], held[kind, chunk, 1, rows, near]
                s = dot_t(q, k) * scale
                if mask == "low":
                    s = jnp.where(col <= row, s, NEG)
                elif mask == "up":
                    s = jnp.where(col > row, s, NEG)
                peak = jnp.max(s, axis=1, keepdims=True)
                if kind is not None:
                    peak = peak + bias[kind]
                m_new = peak if m is None else jnp.maximum(m, peak)
                shift = m_new if kind is None else m_new - bias[kind]
                p = jnp.exp2(s - shift)
                total = jnp.sum(p, axis=1, keepdims=True)
                part = dot(p.astype(jnp.bfloat16), v)
                if m is None:
                    l, acc = total, part
                else:
                    alpha = jnp.exp2(m - m_new)
                    l = l * alpha + total
                    acc = acc * alpha + part
                m = m_new
            out_ref[r : r + tq, wide] = (acc / l).astype(out_ref.dtype)


def pair_columns(lane, table, j, width):
    return jnp.where(lane < width, table[:, 2 * j : 2 * j + 1], table[:, 2 * j + 1 : 2 * j + 2])


def local_states(x_ref, bt_ref, end_ref, decay_ref, local, total):
    rows, total_cols = x_ref.shape
    head_count = end_ref.shape[1]
    width = total_cols // head_count
    lane = lax.broadcasted_iota(jnp.int32, (1, 2 * width), 1)
    weights = jnp.exp(end_ref[...])
    for j in range(head_count // 2):
        cs = slice(2 * width * j, 2 * width * (j + 1))
        state = None
        for block in range(rows // Q):
            rs = slice(block * Q, (block + 1) * Q)
            xs = x_ref[rs, cs].astype(jnp.float32) * pair_columns(lane, weights[rs], j, width)
            one = dot(bt_ref[:, rs], xs.astype(jnp.bfloat16))
            local[block, :, cs] = one
            state = one if state is None else state * decay_ref[block : block + 1, cs] + one
        total[:, cs] = state.astype(jnp.bfloat16)


def recurrence(block, x_ref, b_ref, c_ref, cum_ref, cumt_ref, skip_ref, carried_ref, local, decay_ref, out_ref):
    rows, total_cols = x_ref.shape
    head_count = cum_ref.shape[1]
    width = total_cols // head_count
    pair = 2 * width
    lane = lax.broadcasted_iota(jnp.int32, (1, pair), 1)
    low = lax.broadcasted_iota(jnp.int32, (Q, Q), 1) <= lax.broadcasted_iota(jnp.int32, (Q, Q), 0)
    same = (lax.broadcasted_iota(jnp.int32, (pair, pair), 0) < width) == (
        lax.broadcasted_iota(jnp.int32, (pair, pair), 1) < width
    )
    ones = jnp.where(same, 1.0, 0.0).astype(jnp.bfloat16)
    rs = slice(block * Q, (block + 1) * Q)
    c = c_ref[rs, :]
    cross = jnp.where(low, dot_t(c, b_ref[rs, :]), 0.0)
    cum = cum_ref[rs, :]
    grown = jnp.exp(cum)
    for j in range(head_count // 2):
        cs = slice(pair * j, pair * (j + 1))
        x = x_ref[rs, cs]
        intra = []
        for h in (2 * j, 2 * j + 1):
            gap = cum[:, h : h + 1] - cumt_ref[h : h + 1, rs]
            grid = jnp.exp(jnp.minimum(gap, 0.0))
            intra.append(dot((cross * grid).astype(jnp.bfloat16), x))
        carried = carried_ref[:, cs].astype(jnp.float32)
        for b in range(block):
            carried = carried * decay_ref[b : b + 1, cs] + local[b, :, cs]
        high = carried.astype(jnp.bfloat16)
        inter = dot(c, high)
        if block:
            inter = inter + dot(c, (carried - high.astype(jnp.float32)).astype(jnp.bfloat16))
        mixed = (
            jnp.where(lane < width, intra[0], intra[1])
            + inter * pair_columns(lane, grown, j, width)
            + skip_ref[:, cs] * x.astype(jnp.float32)
        )
        square = mixed * mixed
        big = square.astype(jnp.bfloat16)
        small = (square - big.astype(jnp.float32)).astype(jnp.bfloat16)
        mean = (dot(big, ones) + dot(small, ones)) * (1.0 / width)
        out_ref[rs, cs] = (mixed * lax.rsqrt(mean + 1e-05)).astype(out_ref.dtype)


def kernel(
    size, q_ref, k_ref, v_ref, x_ref, b_ref, bt_ref, c_ref, cum_ref, cumt_ref, end_ref, decay_ref,
    dev_ref, skip_ref, attn_ref, rec_ref, held, local, total, got_s, got_d, sum_q, dec_q, far_s,
    far_d, parts, carried, send, recv, send1, recv1, send2, recv2, send3, recv3,
):
    quads = size // 4
    here = lax.axis_index("seq")
    mine = lax.axis_index("groups")
    quad = here // 4
    member = here % 4
    row = member // 2
    core = member % 2
    chunks = k_ref.shape[1] // CHUNK
    group = total.shape[1] // 4
    blocks = x_ref.shape[0] // Q

    def other(d):
        return 2 * (1 - row if d // 2 else row) + (1 - core if d % 2 else core)

    def beside(d):
        return (mine, quad * 4 + other(d))

    def beyond(e):
        return (mine, (quad + e) % quads * 4 + member)

    def copy(src, dst, sender, receiver, device):
        return pltpu.make_async_remote_copy(
            src_ref=src, dst_ref=dst, send_sem=sender, recv_sem=receiver,
            device_id=device, device_id_type=MESH,
        )

    barrier = pltpu.get_barrier_semaphore()
    for d in range(1, 4):
        pl.semaphore_signal(barrier, inc=1, device_id=beside(d), device_id_type=MESH)
    for e in range(1, quads):
        pl.semaphore_signal(barrier, inc=1, device_id=beyond(e), device_id_type=MESH)
    pl.semaphore_wait(barrier, 3 + quads - 1)

    target = {Z: beyond(1), Y: beside(2), A: beside(1), B: beside(1)}

    def move(kind, chunk, part, src):
        return copy(
            src, held.at[kind, chunk, part], send.at[kind, chunk, part],
            recv.at[kind, chunk, part], target[kind],
        )

    def send_own(kind, chunk):
        wide = pl.ds(pl.multiple_of(chunk * CHUNK, CHUNK), CHUNK)
        for part, ref in ((0, k_ref), (1, v_ref)):
            move(kind, chunk, part, ref.at[:, wide]).start()

    def pass_on(kind, chunk, source):
        for part in range(2):
            move(kind, chunk, part, held.at[source, chunk, part]).start()

    def arrived(kind, chunk):
        for part in range(2):
            move(kind, chunk, part, held.at[kind, chunk, part]).wait_recv()

    def offer(chunk):
        send_own(Z, chunk)

        @pl.when(row == 0)
        def _():
            send_own(Y, chunk)

        @pl.when(core == 0)
        def _():
            send_own(B, chunk)

    def relay(chunk):
        arrived(Z, chunk)

        @pl.when(row == 1)
        def _():
            pass_on(Y, chunk, Z)

        @pl.when(core == 1)
        def _():
            pass_on(B, chunk, Z)

    for chunk in range(min(AHEAD, chunks)):
        offer(chunk)

    def columns(which):
        return pl.ds(pl.multiple_of(which * group, group), group)

    local_states(x_ref, bt_ref, end_ref, decay_ref, local, total)

    def to_member(d):
        at = columns(other(d))
        return (
            copy(total.at[:, at], got_s.at[d], send1.at[0, d], recv1.at[0, d], beside(d)),
            copy(dev_ref.at[:, at], got_d.at[d], send1.at[1, d], recv1.at[1, d], beside(d)),
        )

    def to_quad(e):
        return (
            copy(sum_q, far_s.at[e], send2.at[0, e], recv2.at[0, e], beyond(e)),
            copy(dec_q, far_d.at[e], send2.at[1, e], recv2.at[1, e], beyond(e)),
        )

    def to_owner(d):
        return copy(
            parts.at[other(d)], carried.at[:, columns(member)], send3.at[d], recv3.at[d], beside(d)
        )

    for d in range(1, 4):
        for one in to_member(d):
            one.start()
    got_s[0] = total[:, columns(member)]
    got_d[0] = dev_ref[:, columns(member)]
    for d in range(1, 4):
        for one in to_member(d):
            one.wait_recv()

    def slot(j):
        return jnp.abs(j // 2 - row) * 2 + jnp.abs(j % 2 - core)

    def state_of(j):
        return got_s[slot(j)].astype(jnp.float32)

    def decay_of(j):
        return got_d[slot(j)]

    sums = state_of(0)
    decays = decay_of(0)
    for j in range(1, 4):
        sums = sums * decay_of(j)[0:1] + state_of(j)
        decays = decays * decay_of(j)
    sum_q[...] = sums.astype(jnp.bfloat16)
    dec_q[...] = decays
    for e in range(1, quads):
        for one in to_quad(e):
            one.start()

    def spread():
        for e in range(1, quads):
            for one in to_quad(e):
                one.wait_recv()
        entry = jnp.zeros(sum_q.shape, jnp.float32)
        for e in range(quads - 1, 0, -1):
            grown = entry * far_d[e][0:1] + far_s[e].astype(jnp.float32)
            entry = jnp.where(quad >= e, grown, entry)
        for j in range(4):
            parts[j] = entry.astype(jnp.bfloat16)
            if j < 3:
                entry = entry * decay_of(j)[0:1] + state_of(j)
        for d in range(1, 4):
            to_owner(d).start()
        carried[:, columns(member)] = parts[member]

    def finish(block):
        recurrence(
            block, x_ref, b_ref, c_ref, cum_ref, cumt_ref, skip_ref, carried, local, decay_ref, rec_ref
        )

    def off(seen):
        return jnp.where(seen, 0.0, NEG).astype(jnp.float32)

    inside = quad > 0
    bias = {
        Z: off(inside),
        Y: off(inside | (row == 1)),
        A: off(inside | (row == 1)),
        B: off(inside | (core == 1)),
    }

    relay(0)

    def step(j, carry):
        @pl.when(j + AHEAD < chunks)
        def _():
            offer(j + AHEAD)

        @pl.when(j + 1 < chunks)
        def _():
            relay(j + 1)

        @pl.when(j < chunks)
        def _():
            arrived(Y, j)
            pass_on(A, j, Y)

        @pl.when(j > 0)
        def _():
            arrived(A, j - 1)
            arrived(B, j - 1)
            attend(bias, q_ref, k_ref, v_ref, held, attn_ref, j - 1)

        @pl.when(j == 2)
        def _():
            spread()

        for block in range(blocks):

            @pl.when(j == min(4 + block, chunks))
            def _():
                if block == 0:
                    for d in range(1, 4):
                        copy(
                            parts.at[other(d)], carried.at[:, columns(other(d))], send3.at[d],
                            recv3.at[d], beside(d),
                        ).wait_recv()
                finish(block)

        return carry

    lax.fori_loop(0, chunks + 1, step, 0)

    for d in range(1, 4):
        for one in to_member(d):
            one.wait_send()
        to_owner(d).wait_send()
    for e in range(1, quads):
        for one in to_quad(e):
            one.wait_send()

    def drain(j, carry):
        for kind in range(4):
            for part in range(2):
                move(kind, j, part, held.at[kind, j, part]).wait_send()
        return carry

    lax.fori_loop(0, chunks, drain, 0)


def on_device(queries, keys, values, ssd_input, bmat, cmat, expo, rate, skip):
    length, total_cols = queries.shape
    size = lax.axis_size("seq")
    head_count = rate.shape[0]
    x_cols = ssd_input.shape[1]
    width = x_cols // head_count
    blocks = length // Q
    state = cmat.shape[1]
    group = x_cols // 4
    quads = size // 4
    chunks = total_cols // CHUNK

    loga = -rate[None, :] * expo.astype(jnp.float32)
    cum3 = jnp.cumsum(loga.reshape(blocks, Q, head_count), axis=1)
    ends = cum3[:, -1, :]
    cum = cum3.reshape(length, head_count)
    end_gap = (ends[:, None, :] - cum3).reshape(length, head_count)
    decay_cols = jnp.repeat(jnp.exp(ends), width, axis=1)
    dev = jnp.broadcast_to(jnp.prod(decay_cols, axis=0, keepdims=True), (8, x_cols))
    args = (
        queries, keys, values, ssd_input, bmat, bmat.T, cmat, cum, cum.T, end_gap, decay_cols, dev,
        jnp.repeat(skip, width)[None, :],
    )
    vmem = pl.BlockSpec(memory_space=pltpu.VMEM)
    dma = pltpu.SemaphoreType.DMA
    return pl.pallas_call(
        functools.partial(kernel, size),
        in_specs=[vmem] * len(args),
        out_specs=(vmem, vmem),
        out_shape=(
            jax.ShapeDtypeStruct(queries.shape, jnp.bfloat16),
            jax.ShapeDtypeStruct(ssd_input.shape, jnp.bfloat16),
        ),
        scratch_shapes=[
            pltpu.VMEM((4, chunks, 2, length, CHUNK), jnp.bfloat16),
            pltpu.VMEM((blocks, state, x_cols), jnp.float32),
            pltpu.VMEM((state, x_cols), jnp.bfloat16),
            pltpu.VMEM((4, state, group), jnp.bfloat16),
            pltpu.VMEM((4, 8, group), jnp.float32),
            pltpu.VMEM((state, group), jnp.bfloat16),
            pltpu.VMEM((8, group), jnp.float32),
            pltpu.VMEM((quads, state, group), jnp.bfloat16),
            pltpu.VMEM((quads, 8, group), jnp.float32),
            pltpu.VMEM((4, state, group), jnp.bfloat16),
            pltpu.VMEM((state, x_cols), jnp.bfloat16),
            dma((4, chunks, 2)),
            dma((4, chunks, 2)),
            dma((2, 4)),
            dma((2, 4)),
            dma((2, quads)),
            dma((2, quads)),
            dma((4,)),
            dma((4,)),
        ],
        compiler_params=pltpu.CompilerParams(
            collective_id=0, has_side_effects=True, vmem_limit_bytes=58 << 20
        ),
        name="attention_and_recurrence",
    )(*args)


def solution(mesh):
    split = P(("groups", "seq"), None)
    return jax.shard_map(
        on_device,
        mesh=mesh,
        in_specs=(split,) * 7 + (P(), P()),
        out_specs=(split, split),
        check_vma=False,
    )
```

```python
import functools
import math

import jax
import jax.numpy as jnp
from jax import lax
from jax.experimental import pallas as pl
from jax.experimental.pallas import tpu as pltpu
from jax.sharding import PartitionSpec as P

E = 128
W = 2048
Q = 256
CHUNK = 256
NEG = -1e30
LOG2E = math.log2(math.e)
MESH = pl.DeviceIdType.MESH
Z, Y, A, B = range(4)


def dot(a, b):
    return jnp.dot(a, b, preferred_element_type=jnp.float32)


def dot_t(a, b):
    return lax.dot_general(a, b, (((1,), (1,)), ((), ())), preferred_element_type=jnp.float32)


def attend(bias, q_ref, ko_ref, vo_ref, held, out_ref, chunk):
    length = q_ref.shape[0]
    tq = min(256, length)
    scale = LOG2E / math.sqrt(E)
    row = lax.broadcasted_iota(jnp.int32, (tq, tq), 0)
    col = lax.broadcasted_iota(jnp.int32, (tq, tq), 1)
    for head in range(CHUNK // E):
        wide = pl.ds(pl.multiple_of(chunk * CHUNK + head * E, E), E)
        near = slice(head * E, (head + 1) * E)
        for r in range(0, length, tq):
            q = q_ref[r : r + tq, wide]
            tiles = [(None, r, tq, "low")]
            if r > 0:
                tiles.append((None, 0, r, None))
            tiles.append((Z, r, tq, "up"))
            if r + tq < length:
                tiles.append((Z, r + tq, length - r - tq, None))
            tiles += [(n, 0, length, None) for n in (Y, A, B)]
            m = l = acc = None
            for kind, start, size, mask in tiles:
                rows = slice(start, start + size)
                if kind is None:
                    k, v = ko_ref[rows, wide], vo_ref[rows, wide]
                else:
                    k, v = held[kind, chunk, 0, rows, near], held[kind, chunk, 1, rows, near]
                s = dot_t(q, k) * scale
                if mask == "low":
                    s = jnp.where(col <= row, s, NEG)
                elif mask == "up":
                    s = jnp.where(col > row, s, NEG)
                peak = jnp.max(s, axis=1, keepdims=True)
                if kind is not None:
                    peak = peak + bias[kind]
                m_new = peak if m is None else jnp.maximum(m, peak)
                shift = m_new if kind is None else m_new - bias[kind]
                p = jnp.exp2(s - shift)
                total = jnp.sum(p, axis=1, keepdims=True)
                part = dot(p.astype(jnp.bfloat16), v)
                if m is None:
                    l, acc = total, part
                else:
                    alpha = jnp.exp2(m - m_new)
                    l = l * alpha + total
                    acc = acc * alpha + part
                m = m_new
            out_ref[r : r + tq, wide] = (acc / l).astype(out_ref.dtype)


def pair_columns(lane, table, j, width):
    return jnp.where(lane < width, table[:, 2 * j : 2 * j + 1], table[:, 2 * j + 1 : 2 * j + 2])


def local_states(x_ref, bt_ref, end_ref, decay_ref, local, total):
    rows, total_cols = x_ref.shape
    head_count = end_ref.shape[1]
    width = total_cols // head_count
    lane = lax.broadcasted_iota(jnp.int32, (1, 2 * width), 1)
    weights = jnp.exp(end_ref[...])
    for j in range(head_count // 2):
        cs = slice(2 * width * j, 2 * width * (j + 1))
        state = None
        for block in range(rows // Q):
            rs = slice(block * Q, (block + 1) * Q)
            xs = x_ref[rs, cs].astype(jnp.float32) * pair_columns(lane, weights[rs], j, width)
            one = dot(bt_ref[:, rs], xs.astype(jnp.bfloat16))
            local[block, :, cs] = one
            state = one if state is None else state * decay_ref[block : block + 1, cs] + one
        total[:, cs] = state.astype(jnp.bfloat16)


def recurrence(block, x_ref, b_ref, c_ref, cum_ref, cumt_ref, skip_ref, carried_ref, local, decay_ref, out_ref):
    rows, total_cols = x_ref.shape
    head_count = cum_ref.shape[1]
    width = total_cols // head_count
    pair = 2 * width
    lane = lax.broadcasted_iota(jnp.int32, (1, pair), 1)
    low = lax.broadcasted_iota(jnp.int32, (Q, Q), 1) <= lax.broadcasted_iota(jnp.int32, (Q, Q), 0)
    same = (lax.broadcasted_iota(jnp.int32, (pair, pair), 0) < width) == (
        lax.broadcasted_iota(jnp.int32, (pair, pair), 1) < width
    )
    ones = jnp.where(same, 1.0, 0.0).astype(jnp.bfloat16)
    rs = slice(block * Q, (block + 1) * Q)
    c = c_ref[rs, :]
    cross = jnp.where(low, dot_t(c, b_ref[rs, :]), 0.0)
    cum = cum_ref[rs, :]
    grown = jnp.exp(cum)
    for j in range(head_count // 2):
        cs = slice(pair * j, pair * (j + 1))
        x = x_ref[rs, cs]
        intra = []
        for h in (2 * j, 2 * j + 1):
            gap = cum[:, h : h + 1] - cumt_ref[h : h + 1, rs]
            grid = jnp.exp(jnp.minimum(gap, 0.0))
            intra.append(dot((cross * grid).astype(jnp.bfloat16), x))
        carried = carried_ref[:, cs].astype(jnp.float32)
        for b in range(block):
            carried = carried * decay_ref[b : b + 1, cs] + local[b, :, cs]
        high = carried.astype(jnp.bfloat16)
        inter = dot(c, high)
        if block:
            inter = inter + dot(c, (carried - high.astype(jnp.float32)).astype(jnp.bfloat16))
        mixed = (
            jnp.where(lane < width, intra[0], intra[1])
            + inter * pair_columns(lane, grown, j, width)
            + skip_ref[:, cs] * x.astype(jnp.float32)
        )
        square = mixed * mixed
        big = square.astype(jnp.bfloat16)
        small = (square - big.astype(jnp.float32)).astype(jnp.bfloat16)
        mean = (dot(big, ones) + dot(small, ones)) * (1.0 / width)
        out_ref[rs, cs] = (mixed * lax.rsqrt(mean + 1e-05)).astype(out_ref.dtype)


def kernel(
    size, q_ref, k_ref, v_ref, x_ref, b_ref, bt_ref, c_ref, cum_ref, cumt_ref, end_ref, decay_ref,
    dev_ref, skip_ref, attn_ref, rec_ref, held, local, total, got_s, got_d, sum_q, dec_q, far_s,
    far_d, parts, carried, send, recv, send1, recv1, send2, recv2, send3, recv3,
):
    quads = size // 4
    here = lax.axis_index("seq")
    mine = lax.axis_index("groups")
    quad = here // 4
    member = here % 4
    row = member // 2
    core = member % 2
    chunks = k_ref.shape[1] // CHUNK
    group = total.shape[1] // 4
    blocks = x_ref.shape[0] // Q

    def other(d):
        return 2 * (1 - row if d // 2 else row) + (1 - core if d % 2 else core)

    def beside(d):
        return (mine, quad * 4 + other(d))

    def beyond(e):
        return (mine, (quad + e) % quads * 4 + member)

    def copy(src, dst, sender, receiver, device):
        return pltpu.make_async_remote_copy(
            src_ref=src, dst_ref=dst, send_sem=sender, recv_sem=receiver,
            device_id=device, device_id_type=MESH,
        )

    barrier = pltpu.get_barrier_semaphore()
    for d in range(1, 4):
        pl.semaphore_signal(barrier, inc=1, device_id=beside(d), device_id_type=MESH)
    for e in range(1, quads):
        pl.semaphore_signal(barrier, inc=1, device_id=beyond(e), device_id_type=MESH)
    pl.semaphore_wait(barrier, 3 + quads - 1)

    target = {Z: beyond(1), Y: beside(2), A: beside(1), B: beside(1)}

    def move(kind, chunk, part, src):
        return copy(
            src, held.at[kind, chunk, part], send.at[kind, chunk, part],
            recv.at[kind, chunk, part], target[kind],
        )

    def send_own(kind, chunk):
        wide = pl.ds(pl.multiple_of(chunk * CHUNK, CHUNK), CHUNK)
        for part, ref in ((0, k_ref), (1, v_ref)):
            move(kind, chunk, part, ref.at[:, wide]).start()

    def pass_on(kind, chunk, source):
        for part in range(2):
            move(kind, chunk, part, held.at[source, chunk, part]).start()

    def arrived(kind, chunk):
        for part in range(2):
            move(kind, chunk, part, held.at[kind, chunk, part]).wait_recv()

    def offer(chunk):
        send_own(Z, chunk)

        @pl.when(core == 0)
        def _():
            send_own(B, chunk)

    def relay(chunk):
        @pl.when(row == 0)
        def _():
            send_own(Y, chunk)

        arrived(Z, chunk)

        @pl.when(row == 1)
        def _():
            pass_on(Y, chunk, Z)

        @pl.when(core == 1)
        def _():
            pass_on(B, chunk, Z)

    ahead = 2 - core
    offer(0)

    @pl.when(core == 0)
    def _():
        offer(1)

    def columns(which):
        return pl.ds(pl.multiple_of(which * group, group), group)

    local_states(x_ref, bt_ref, end_ref, decay_ref, local, total)

    def to_member(d):
        at = columns(other(d))
        return (
            copy(total.at[:, at], got_s.at[d], send1.at[0, d], recv1.at[0, d], beside(d)),
            copy(dev_ref.at[:, at], got_d.at[d], send1.at[1, d], recv1.at[1, d], beside(d)),
        )

    def to_quad(e):
        return (
            copy(sum_q, far_s.at[e], send2.at[0, e], recv2.at[0, e], beyond(e)),
            copy(dec_q, far_d.at[e], send2.at[1, e], recv2.at[1, e], beyond(e)),
        )

    def to_owner(d):
        return copy(
            parts.at[other(d)], carried.at[:, columns(member)], send3.at[d], recv3.at[d], beside(d)
        )

    for d in range(1, 4):
        for one in to_member(d):
            one.start()
    got_s[0] = total[:, columns(member)]
    got_d[0] = dev_ref[:, columns(member)]
    for d in range(1, 4):
        for one in to_member(d):
            one.wait_recv()

    def slot(j):
        return jnp.abs(j // 2 - row) * 2 + jnp.abs(j % 2 - core)

    def state_of(j):
        return got_s[slot(j)].astype(jnp.float32)

    def decay_of(j):
        return got_d[slot(j)]

    sums = state_of(0)
    decays = decay_of(0)
    for j in range(1, 4):
        sums = sums * decay_of(j)[0:1] + state_of(j)
        decays = decays * decay_of(j)
    sum_q[...] = sums.astype(jnp.bfloat16)
    dec_q[...] = decays
    for e in range(1, quads):
        for one in to_quad(e):
            one.start()

    def spread():
        for e in range(1, quads):
            for one in to_quad(e):
                one.wait_recv()
        entry = jnp.zeros(sum_q.shape, jnp.float32)
        for e in range(quads - 1, 0, -1):
            grown = entry * far_d[e][0:1] + far_s[e].astype(jnp.float32)
            entry = jnp.where(quad >= e, grown, entry)
        for j in range(4):
            parts[j] = entry.astype(jnp.bfloat16)
            if j < 3:
                entry = entry * decay_of(j)[0:1] + state_of(j)
        for d in range(1, 4):
            to_owner(d).start()
        carried[:, columns(member)] = parts[member]

    def finish(block):
        recurrence(
            block, x_ref, b_ref, c_ref, cum_ref, cumt_ref, skip_ref, carried, local, decay_ref, rec_ref
        )

    def off(seen):
        return jnp.where(seen, 0.0, NEG).astype(jnp.float32)

    inside = quad > 0
    bias = {
        Z: off(inside),
        Y: off(inside | (row == 1)),
        A: off(inside | (row == 1)),
        B: off(inside | (core == 1)),
    }

    relay(0)
    offer(ahead)

    def step(j, carry):
        @pl.when(j + 1 < chunks)
        def _():
            relay(j + 1)

        @pl.when(j + 1 + ahead < chunks)
        def _():
            offer(j + 1 + ahead)

        @pl.when(j < chunks)
        def _():
            arrived(Y, j)
            pass_on(A, j, Y)

        @pl.when(j > 0)
        def _():
            arrived(A, j - 1)
            arrived(B, j - 1)
            attend(bias, q_ref, k_ref, v_ref, held, attn_ref, j - 1)

        @pl.when(j == 2)
        def _():
            spread()

        for block in range(blocks):

            @pl.when(j == min(4 + block, chunks))
            def _():
                if block == 0:
                    for d in range(1, 4):
                        copy(
                            parts.at[other(d)], carried.at[:, columns(other(d))], send3.at[d],
                            recv3.at[d], beside(d),
                        ).wait_recv()
                finish(block)

        return carry

    lax.fori_loop(0, chunks + 1, step, 0)

    for d in range(1, 4):
        for one in to_member(d):
            one.wait_send()
        to_owner(d).wait_send()
    for e in range(1, quads):
        for one in to_quad(e):
            one.wait_send()

    def drain(j, carry):
        for kind in range(4):
            for part in range(2):
                move(kind, j, part, held.at[kind, j, part]).wait_send()
        return carry

    lax.fori_loop(0, chunks, drain, 0)


def on_device(queries, keys, values, ssd_input, bmat, cmat, expo, rate, skip):
    length, total_cols = queries.shape
    size = lax.axis_size("seq")
    head_count = rate.shape[0]
    x_cols = ssd_input.shape[1]
    width = x_cols // head_count
    blocks = length // Q
    state = cmat.shape[1]
    group = x_cols // 4
    quads = size // 4
    chunks = total_cols // CHUNK

    loga = -rate[None, :] * expo.astype(jnp.float32)
    cum3 = jnp.cumsum(loga.reshape(blocks, Q, head_count), axis=1)
    ends = cum3[:, -1, :]
    cum = cum3.reshape(length, head_count)
    end_gap = (ends[:, None, :] - cum3).reshape(length, head_count)
    decay_cols = jnp.repeat(jnp.exp(ends), width, axis=1)
    dev = jnp.broadcast_to(jnp.prod(decay_cols, axis=0, keepdims=True), (8, x_cols))
    args = (
        queries, keys, values, ssd_input, bmat, bmat.T, cmat, cum, cum.T, end_gap, decay_cols, dev,
        jnp.repeat(skip, width)[None, :],
    )
    vmem = pl.BlockSpec(memory_space=pltpu.VMEM)
    dma = pltpu.SemaphoreType.DMA
    return pl.pallas_call(
        functools.partial(kernel, size),
        in_specs=[vmem] * len(args),
        out_specs=(vmem, vmem),
        out_shape=(
            jax.ShapeDtypeStruct(queries.shape, jnp.bfloat16),
            jax.ShapeDtypeStruct(ssd_input.shape, jnp.bfloat16),
        ),
        scratch_shapes=[
            pltpu.VMEM((4, chunks, 2, length, CHUNK), jnp.bfloat16),
            pltpu.VMEM((blocks, state, x_cols), jnp.float32),
            pltpu.VMEM((state, x_cols), jnp.bfloat16),
            pltpu.VMEM((4, state, group), jnp.bfloat16),
            pltpu.VMEM((4, 8, group), jnp.float32),
            pltpu.VMEM((state, group), jnp.bfloat16),
            pltpu.VMEM((8, group), jnp.float32),
            pltpu.VMEM((quads, state, group), jnp.bfloat16),
            pltpu.VMEM((quads, 8, group), jnp.float32),
            pltpu.VMEM((4, state, group), jnp.bfloat16),
            pltpu.VMEM((state, x_cols), jnp.bfloat16),
            dma((4, chunks, 2)),
            dma((4, chunks, 2)),
            dma((2, 4)),
            dma((2, 4)),
            dma((2, quads)),
            dma((2, quads)),
            dma((4,)),
            dma((4,)),
        ],
        compiler_params=pltpu.CompilerParams(
            collective_id=0, has_side_effects=True, vmem_limit_bytes=58 << 20
        ),
        name="attention_and_recurrence",
    )(*args)


def solution(mesh):
    split = P(("groups", "seq"), None)
    return jax.shard_map(
        on_device,
        mesh=mesh,
        in_specs=(split,) * 7 + (P(), P()),
        out_specs=(split, split),
        check_vma=False,
    )
```
